1024 devices in a mesh: row: 64 (over z, y_hi), col: 16 (over y_lo, x, core).
Axes of the slice: x: 4, y: 4 (y_hi: 2, y_lo: 2; y = y_hi * 2 + y_lo), z: 32, core: 2. Of those that a mesh axis runs over, the one named last changes fastest.
Arguments:
- valence_pairs: bfloat16 [128, 128, 1024], P('row', 'col'), may hold values from -0.09375 to 0.09375
- conduction_pairs: bfloat16 [192, 192, 1024], P('row', 'col'), may hold values from -0.09375 to 0.09375
- screening: bfloat16 [1024, 1024], replicated, may hold values from -0.0390625 to 1.5
- valence_energy: float32 [128], P('col'), may hold values from -2 to 0
- conduction_energy: float32 [192], P('row'), may hold values from 3 to 6
- vectors: bfloat16 [192, 128, 128], P('row', 'col'), may hold values from -6 to 6
Outputs:
- first_step: bfloat16 [192, 128, 128], P('row', 'col')
- filtered: float32 [192, 128, 128], P('row', 'col')
The draws below stay inside these ranges and needn't reach their ends.
All inputs are finite; a program needn't handle non-finite values.
Results may differ from the reference program's by a relative error of at most 0.0043.
Values may be sent and summed in bfloat16 or wider, within the bound.
A program may use at most 64 MiB of HBM per device.

```python
import math
import jax
import jax.numpy as jnp
from jax import lax

NV = 128
NC = 192
NAUX = 1024
M = 128


def draw_screening(key, part):
    key_diag = jax.random.fold_in(key, 11)
    key_off = jax.random.fold_in(key, 23)
    indices = jnp.arange(NAUX)
    identity = (indices[:, None] == indices[None, :]).astype(jnp.float32)
    bound = 1.25 / math.sqrt(NAUX)
    diagonal = jax.random.uniform(key_diag, (NAUX,), jnp.float32, 0.6, 1.4)
    offdiag = jnp.clip(jax.random.normal(key_off, (NAUX, NAUX), jnp.float32), -2.5, 2.5) * (bound / 2.5)
    matrix = identity * diagonal[None, :] + (1.0 - identity) * offdiag
    return matrix.astype(jnp.bfloat16)


def steps_of(stream_key, dims, shards, low, top_value):
    loudness, own = 1.0, jax.random.fold_in(stream_key, 6)
    for position, parts in shards:
        heights = jnp.exp(jax.random.uniform(jax.random.fold_in(own, position), (parts,), jnp.float32, low / len(shards), top_value / len(shards)))
        loudness = loudness * jnp.repeat(heights, dims[position] // parts).reshape([-1 if axis == position else 1 for axis in range(len(dims))])
    return loudness


def noise(rng, extent, scale, most, split=(), kind=jnp.bfloat16):
    values = scale * jax.random.normal(rng, extent, jnp.float32)
    if split:
        values = values * steps_of(rng, extent, split, -0.22, 0.18)
    return jnp.clip(values, -most, most).astype(kind)


def setup_inputs(seed: int = 0) -> dict:
    keys = jax.random.split(jax.random.key(seed), 7)
    valence_pairs = noise(keys[0], (NV, NV, NAUX), (1.1 * (NV * NC * NAUX) ** -0.25), 0.09375, ((0, 64), (1, 16)))
    conduction_pairs = noise(keys[1], (NC, NC, NAUX), (1.1 * (NV * NC * NAUX) ** -0.25), 0.09375, ((0, 64), (1, 16)))
    screening = draw_screening(jax.random.fold_in(keys[6], 71), 0)
    valence_energy = jnp.clip(-2.0 + 2.0 * jax.random.uniform(keys[3], (NV,), jnp.float32) ** steps_of(keys[3], (NV,), ((0, 16),), -0.2, 0.2), -2.0, 0.0)
    conduction_energy = jnp.clip(3.0 + 3.0 * jax.random.uniform(keys[4], (NC,), jnp.float32) ** steps_of(keys[4], (NC,), ((0, 64),), -0.2, 0.2), 3.0, 6.0)
    vectors = noise(keys[5], (NC, NV, M), 1.0, 6.0, ((0, 64), (1, 16)))
    return dict(valence_pairs=valence_pairs, conduction_pairs=conduction_pairs, screening=screening, valence_energy=valence_energy, conduction_energy=conduction_energy, vectors=vectors)


shift_center = 5.5
half_width = 3.0
aux_step = 16


def screened_valence(valence_pairs, screening):
    flattened = valence_pairs.reshape(NV * NV, NAUX)
    product = jnp.dot(flattened, screening, preferred_element_type=jnp.float32)
    return product.astype(jnp.bfloat16).reshape(NV, NV, NAUX)


def kernel_action(screened, conduction_pairs, current):
    groups = NAUX // aux_step
    valence_blocks = jnp.transpose(screened.astype(jnp.float32), (2, 0, 1)).reshape(groups, aux_step, NV, NV)
    conduction_blocks = jnp.transpose(conduction_pairs.astype(jnp.float32), (2, 0, 1)).reshape(groups, aux_step, NC, NC)

    def accumulate(running, blocks):
        valence_part, conduction_part = blocks
        halfway = jnp.einsum("pcd,dwk->pcwk", conduction_part, current, precision=lax.Precision.HIGHEST)
        running = running + jnp.einsum("pvw,pcwk->cvk", valence_part, halfway, precision=lax.Precision.HIGHEST)
        return running, None

    initial = jnp.zeros((NC, NV, current.shape[2]), jnp.float32)
    running, unused = lax.scan(accumulate, initial, (valence_blocks, conduction_blocks))
    return running


def reference(valence_pairs, conduction_pairs, screening, valence_energy, conduction_energy, vectors):
    screened = screened_valence(valence_pairs, screening)
    energy_gaps = (conduction_energy[:, None] - valence_energy[None, :] - shift_center)[:, :, None]

    def operator(current):
        coupled = kernel_action(screened, conduction_pairs, current)
        return (energy_gaps * current - coupled) / half_width

    starting = vectors.astype(jnp.float32)
    first_step = operator(starting).astype(jnp.bfloat16)
    filtered = 2.0 * operator(first_step.astype(jnp.float32)) - starting
    return first_step, filtered
```

```python
import jax
import jax.numpy as jnp
from jax import lax
from jax.sharding import PartitionSpec as P

shift_center = 5.5
half_width = 3.0


def screen_rows(portion, screening):
    aux_width = portion.shape[2]
    flattened = portion.reshape(-1, aux_width)
    product = jnp.dot(flattened, screening, preferred_element_type=jnp.float32)
    return product.astype(jnp.bfloat16).reshape(portion.shape)


def on_device(
    valence_pairs, conduction_pairs, screening, valence_energy, conduction_energy, vectors
):
    screened = lax.all_gather(screen_rows(valence_pairs, screening), "row", axis=0, tiled=True)
    kernel_tile = jnp.einsum(
        "vwp,cdp->cvwd",
        screened,
        lax.all_gather(conduction_pairs, "col", axis=1, tiled=True),
        preferred_element_type=jnp.float32,
    ).astype(jnp.bfloat16)
    energy_gaps = (conduction_energy[:, None] - valence_energy[None, :] - shift_center)[:, :, None]

    def operator(current):
        partial_sum = jnp.einsum(
            "cvwd,dwk->cvk",
            kernel_tile,
            lax.all_gather(current, "row", axis=0, tiled=True),
            preferred_element_type=jnp.float32,
        )
        coupled = lax.psum_scatter(partial_sum, "col", scatter_dimension=1, tiled=True)
        return (energy_gaps * current.astype(jnp.float32) - coupled) / half_width

    first_step = operator(vectors).astype(jnp.bfloat16)
    filtered = 2.0 * operator(first_step) - vectors.astype(jnp.float32)
    return (first_step, filtered)


def solution(mesh):
    return jax.shard_map(
        on_device,
        mesh=mesh,
        in_specs=(
            P("row", "col", None),
            P("row", "col", None),
            P(),
            P("col"),
            P("row"),
            P("row", "col", None),
        ),
        out_specs=(P("row", "col", None), P("row", "col", None)),
        check_vma=False,
    )
```

```python
import jax
import jax.numpy as jnp
from jax import lax
from jax.experimental import pallas as pl
from jax.experimental.pallas import tpu as pltpu
from jax.sharding import PartitionSpec as P

shift_center = 5.5
half_width = 3.0

NZ = 32
NQ = 16
NPLANE = 32
FAR = (16, 12, 20, 8, 24, 4, 28)
NEAR = (1, 31, 2)
GREETED = (1, 2, 4, 8, 12, 16, 20, 24, 28, 30, 31)
MESH = pl.DeviceIdType.MESH


def body(
    v_ref, c_ref, screening_ref, gaps_ref, u_ref,
    first_ref, filtered_ref,
    v_both, screen_half, s_ring, s_wide, s_rows, c_all, k_tile,
    u_one, u_two, u_wide, u_rows, y_part, y_two, r_one, r_two,
    local_sem, v_sem, c_send, c_recv, right_send, right_recv, left_send, left_recv,
    gather_send, gather_recv, sum_send, sum_recv,
):
    row = lax.axis_index("row")
    q = lax.axis_index("col")
    z = row // 2
    y = row % 2
    me = y * NQ + q
    z_class = z % 4
    z_step = z // 4

    def plane_id(i):
        p = (me + i) % NPLANE
        return p // NQ, p % NQ

    def z_id(distance):
        return (((z + distance) % NZ) * 2 + y, q)

    barrier = pltpu.get_barrier_semaphore()

    @pl.loop(1, NPLANE)
    def _(i):
        ty, tq = plane_id(i)
        pl.semaphore_signal(barrier, inc=1, device_id=(z * 2 + ty, tq), device_id_type=MESH)

    for distance in GREETED:
        pl.semaphore_signal(barrier, inc=1, device_id=z_id(distance), device_id_type=MESH)

    screen_copy = pltpu.make_async_copy(
        screening_ref.at[:, pl.ds(pl.multiple_of(y * 512, 512), 512)], screen_half, local_sem.at[0]
    )
    screen_copy.start()
    own_c = pltpu.make_async_copy(
        c_ref.at[y],
        c_all.at[pl.ds(y * 3, 3), pl.ds(pl.multiple_of(q * 16, 16), 16), :],
        local_sem.at[1],
    )
    own_c.start()
    u_wide[...] = jnp.zeros_like(u_wide)
    u_one[z_class, z_step, y] = u_ref[...]
    pl.semaphore_wait(barrier, NPLANE - 1 + len(GREETED))

    partner = ((z * 2 + 1 - y), q)
    v_copy = pltpu.make_async_remote_copy(
        src_ref=v_ref, dst_ref=v_both.at[y], send_sem=v_sem.at[0], recv_sem=v_sem.at[1],
        device_id=partner, device_id_type=MESH,
    )
    v_copy.start()

    def pair_copy(buf, op):
        return pltpu.make_async_remote_copy(
            src_ref=buf.at[z_class, z_step, y], dst_ref=buf.at[z_class, z_step, y],
            send_sem=gather_send.at[op, 0], recv_sem=gather_recv.at[op, 0],
            device_id=partner, device_id_type=MESH,
        )

    def far_copy(buf, op, n):
        return pltpu.make_async_remote_copy(
            src_ref=buf.at[z_class, z_step], dst_ref=buf.at[z_class, z_step],
            send_sem=gather_send.at[op, 1 + n], recv_sem=gather_recv.at[op, 1 + n],
            device_id=z_id(FAR[n]), device_id_type=MESH,
        )

    def near_copy(buf, op, n):
        return pltpu.make_async_remote_copy(
            src_ref=buf.at[z_class], dst_ref=buf.at[z_class],
            send_sem=gather_send.at[op, 8 + n], recv_sem=gather_recv.at[op, 8 + n],
            device_id=z_id(NEAR[n]), device_id_type=MESH,
        )

    pair_copy(u_one, 0).start()

    def c_copy(i):
        ty, tq = plane_id(i)
        return pltpu.make_async_remote_copy(
            src_ref=c_ref.at[ty],
            dst_ref=c_all.at[pl.ds(y * 3, 3), pl.ds(pl.multiple_of(q * 16, 16), 16), :],
            send_sem=c_send.at[i], recv_sem=c_recv.at[i],
            device_id=(z * 2 + ty, tq), device_id_type=MESH,
        )

    v_both[y] = v_ref[...]

    @pl.loop(1, NPLANE)
    def _(i):
        c_copy(i).start()

    screen_copy.wait()
    v_copy.wait()
    raw = v_both[...].astype(jnp.float32).reshape(32, 1024).astype(jnp.bfloat16)
    s_ring[z] = jnp.dot(raw, screen_half[...], preferred_element_type=jnp.float32).astype(jnp.bfloat16)

    def right_copy(s):
        block = (z + NZ - s) % NZ
        return pltpu.make_async_remote_copy(
            src_ref=s_ring.at[block], dst_ref=s_ring.at[block],
            send_sem=right_send.at[s], recv_sem=right_recv.at[s],
            device_id=z_id(1), device_id_type=MESH,
        )

    def left_copy(s):
        block = (z + s) % NZ
        return pltpu.make_async_remote_copy(
            src_ref=s_ring.at[block], dst_ref=s_ring.at[block],
            send_sem=left_send.at[s], recv_sem=left_recv.at[s],
            device_id=z_id(NZ - 1), device_id_type=MESH,
        )

    def widen(block):
        rows = s_ring[block].astype(jnp.float32)
        for j in range(4):
            s_wide[j, pl.ds(pl.multiple_of(block * 32, 32), 32), :] = rows[:, j * 128:(j + 1) * 128]

    def ring_step(s):
        right_copy(s).start()
        left_copy(s).start()
        widen((z + NZ - s) % NZ)
        widen((z + s) % NZ)
        right_copy(s).wait_recv()
        left_copy(s).wait_recv()

    right_copy(0).start()
    left_copy(0).start()
    pair_copy(u_one, 0).wait()
    for n in range(len(FAR)):
        far_copy(u_one, 0, n).start()
    widen(z)
    right_copy(0).wait_recv()
    left_copy(0).wait_recv()

    @pl.loop(1, 9)
    def _(s):
        ring_step(s)

    for n in range(len(FAR)):
        far_copy(u_one, 0, n).wait()
    for n in range(len(NEAR)):
        near_copy(u_one, 0, n).start()

    @pl.loop(9, 15)
    def _(s):
        ring_step(s)

    right_copy(15).start()
    widen((z + 17) % NZ)
    widen((z + 15) % NZ)
    right_copy(15).wait_recv()
    widen((z + 16) % NZ)

    @pl.loop(0, 8)
    def _(w):
        for j in range(4):
            s_rows[w, :, j * 128:(j + 1) * 128] = s_wide[j, pl.ds(w, 128, stride=8), :].astype(jnp.bfloat16)

    own_c.wait()

    @pl.loop(1, NPLANE)
    def _(i):
        c_copy(i).wait()

    @pl.loop(0, 6)
    def _(c):
        conduction = c_all[c]
        for w in range(8):
            k_tile[c, :, w * 256:(w + 1) * 256] = lax.dot_general(
                s_rows[w], conduction, (((1,), (1,)), ((), ())), preferred_element_type=jnp.float32
            ).astype(jnp.bfloat16)

    for n in range(len(NEAR)):
        near_copy(u_one, 0, n).wait()

    def products(buf, part):
        for za in range(4):
            for zq in range(8):
                start = (zq * 2 + za // 2) * 128 + (za % 2) * 48
                for half in range(2):
                    u_wide[start + half * 24:start + half * 24 + 24, :] = (
                        buf[za, zq, half].astype(jnp.float32).reshape(24, 128)
                    )

        for w in range(8):
            u_rows[w * 256:(w + 1) * 256, :] = u_wide[pl.ds(w, 256, stride=8), :].astype(jnp.bfloat16)

        @pl.loop(0, 6)
        def _(c):
            part[c] = jnp.dot(k_tile[c], u_rows[...], preferred_element_type=jnp.float32)

    def sum_copy(part, landing, op, i):
        ty, tq = plane_id(i)
        return pltpu.make_async_remote_copy(
            src_ref=part.at[pl.ds(ty * 3, 3), pl.ds(pl.multiple_of(tq * 8, 8), 8), :],
            dst_ref=landing.at[i],
            send_sem=sum_send.at[op, i], recv_sem=sum_recv.at[op, i],
            device_id=(z * 2 + ty, tq), device_id_type=MESH,
        )

    def reduced(part, landing, op):
        @pl.loop(1, NPLANE)
        def _(i):
            sum_copy(part, landing, op, i).start()

        landing[0] = part[pl.ds(y * 3, 3), pl.ds(pl.multiple_of(q * 8, 8), 8), :]

        @pl.loop(1, NPLANE)
        def _(i):
            sum_copy(part, landing, op, i).wait()

        return jnp.sum(landing[...], axis=0)

    products(u_one, y_part)
    start = u_ref[...].astype(jnp.float32)
    first = ((gaps_ref[...] * start - reduced(y_part, r_one, 0)) / half_width).astype(jnp.bfloat16)
    u_two[z_class, z_step, y] = first
    first_ref[...] = first

    pair_copy(u_two, 1).start()
    pair_copy(u_two, 1).wait()
    for n in range(len(FAR)):
        far_copy(u_two, 1, n).start()
    for n in range(len(FAR)):
        far_copy(u_two, 1, n).wait()
    for n in range(len(NEAR)):
        near_copy(u_two, 1, n).start()
    for n in range(len(NEAR)):
        near_copy(u_two, 1, n).wait()

    products(u_two, y_two)
    second = (gaps_ref[...] * first.astype(jnp.float32) - reduced(y_two, r_two, 1)) / half_width
    filtered_ref[...] = 2.0 * second - start

    @pl.loop(0, 15)
    def _(s):
        right_copy(s).wait_send()
        left_copy(s).wait_send()

    right_copy(15).wait_send()


def on_device(
    valence_pairs, conduction_pairs, screening, valence_energy, conduction_energy, vectors
):
    gaps = (conduction_energy[:, None] - valence_energy[None, :] - shift_center)[:, :, None]
    gaps = jnp.broadcast_to(gaps, vectors.shape)
    padded = jnp.pad(conduction_pairs, ((0, 0), (0, 4), (0, 0)))
    halves = jnp.transpose(padded.reshape(3, 16, 2, 512), (2, 0, 1, 3))
    in_vmem = pl.BlockSpec(memory_space=pltpu.VMEM)
    bf16, f32 = jnp.bfloat16, jnp.float32
    dma = pltpu.SemaphoreType.DMA
    return pl.pallas_call(
        body,
        out_shape=(
            jax.ShapeDtypeStruct(vectors.shape, bf16),
            jax.ShapeDtypeStruct(vectors.shape, f32),
        ),
        in_specs=[in_vmem, in_vmem, pl.BlockSpec(memory_space=pl.ANY), in_vmem, in_vmem],
        out_specs=(in_vmem, in_vmem),
        scratch_shapes=[
            pltpu.VMEM((2, 2, 8, 1024), bf16),
            pltpu.VMEM((1024, 512), bf16),
            pltpu.VMEM((NZ, 32, 512), bf16),
            pltpu.VMEM((4, 1024, 128), f32),
            pltpu.VMEM((8, 128, 512), bf16),
            pltpu.VMEM((6, 256, 512), bf16),
            pltpu.VMEM((6, 128, 2048), bf16),
            pltpu.VMEM((4, 8, 2, 3, 8, 128), bf16),
            pltpu.VMEM((4, 8, 2, 3, 8, 128), bf16),
            pltpu.VMEM((2048, 128), f32),
            pltpu.VMEM((2048, 128), bf16),
            pltpu.VMEM((6, 128, 128), f32),
            pltpu.VMEM((6, 128, 128), f32),
            pltpu.VMEM((NPLANE, 3, 8, 128), f32),
            pltpu.VMEM((NPLANE, 3, 8, 128), f32),
            dma((2,)),
            dma((2,)),
            dma((NPLANE,)),
            dma((NPLANE,)),
            dma((16,)),
            dma((16,)),
            dma((16,)),
            dma((16,)),
            dma((2, 11)),
            dma((2, 11)),
            dma((2, NPLANE)),
            dma((2, NPLANE)),
        ],
        compiler_params=pltpu.CompilerParams(collective_id=0, has_side_effects=True),
    )(valence_pairs, halves, screening, gaps, vectors)


def solution(mesh):
    return jax.shard_map(
        on_device,
        mesh=mesh,
        in_specs=(
            P("row", "col", None),
            P("row", "col", None),
            P(),
            P("col"),
            P("row"),
            P("row", "col", None),
        ),
        out_specs=(P("row", "col", None), P("row", "col", None)),
        check_vma=False,
    )
```

```python
import jax
import jax.numpy as jnp
from jax import lax
from jax.experimental import pallas as pl
from jax.experimental.pallas import tpu as pltpu
from jax.sharding import PartitionSpec as P

shift_center = 5.5
half_width = 3.0

NZ = 32
NQ = 16
NPLANE = 32
SEEDS = (0, 24, 8, 16)
SPREAD = (4, 3, 29, 2, 30, 1, 31)
GREETED = (1, 2, 3, 4, 8, 24, 28, 29, 30, 31)
MESH = pl.DeviceIdType.MESH


def body(
    v_ref, c_ref, screening_ref, gaps_ref, u_ref,
    first_ref, filtered_ref,
    screen_own, screen_other, s_pair, s_ring, s_wide, s_rows, c_all, k_tile,
    u_one, u_two, u_wide, u_rows, y_part, y_two, r_one, r_two,
    local_sem, v_sem, c_send, c_recv, far_send, far_recv, ring_send, ring_recv,
    gather_send, gather_recv, sum_send, sum_recv,
):
    row = lax.axis_index("row")
    q = lax.axis_index("col")
    z = row // 2
    y = row % 2
    me = y * NQ + q

    def plane_id(i):
        p = (me + i) % NPLANE
        return p // NQ, p % NQ

    def z_id(distance):
        return (((z + distance) % NZ) * 2 + y, q)

    def block_at(distance):
        return (z + distance) % NZ

    barrier = pltpu.get_barrier_semaphore()

    for distance in GREETED:
        pl.semaphore_signal(barrier, inc=1, device_id=z_id(distance), device_id_type=MESH)

    @pl.loop(1, NPLANE)
    def _(i):
        ty, tq = plane_id(i)
        pl.semaphore_signal(barrier, inc=1, device_id=(z * 2 + ty, tq), device_id_type=MESH)

    def screen_copy(half, buf, n):
        return pltpu.make_async_copy(
            screening_ref.at[:, pl.ds(pl.multiple_of(half * 512, 512), 512)], buf, local_sem.at[n]
        )

    screen_copy(1 - y, screen_other, 0).start()
    screen_copy(y, screen_own, 1).start()
    own_c = pltpu.make_async_copy(
        c_ref.at[y],
        c_all.at[pl.ds(y * 3, 3), pl.ds(pl.multiple_of(q * 16, 16), 16), :],
        local_sem.at[2],
    )
    own_c.start()
    u_wide[...] = jnp.zeros_like(u_wide)
    u_one[z, y] = u_ref[...]

    raw = v_ref[...].astype(jnp.float32).reshape(16, 1024).astype(jnp.bfloat16)
    own_rows = pl.ds(pl.multiple_of(y * 16, 16), 16)
    screen_copy(1 - y, screen_other, 0).wait()
    s_pair[...] = jnp.dot(raw, screen_other[...], preferred_element_type=jnp.float32).astype(jnp.bfloat16)
    screen_copy(y, screen_own, 1).wait()
    s_ring[z, own_rows, :] = jnp.dot(raw, screen_own[...], preferred_element_type=jnp.float32).astype(
        jnp.bfloat16
    )
    pl.semaphore_wait(barrier, NPLANE - 1 + len(GREETED))

    partner = ((z * 2 + 1 - y), q)
    s_copy = pltpu.make_async_remote_copy(
        src_ref=s_pair, dst_ref=s_ring.at[z, own_rows, :], send_sem=v_sem.at[0], recv_sem=v_sem.at[1],
        device_id=partner, device_id_type=MESH,
    )
    s_copy.start()

    def pair_copy(buf, op):
        return pltpu.make_async_remote_copy(
            src_ref=buf.at[z, y], dst_ref=buf.at[z, y],
            send_sem=gather_send.at[op, 0], recv_sem=gather_recv.at[op, 0],
            device_id=partner, device_id_type=MESH,
        )

    def far_copy(buf, op, n):
        return pltpu.make_async_remote_copy(
            src_ref=buf.at[z], dst_ref=buf.at[z],
            send_sem=gather_send.at[op, 1 + n], recv_sem=gather_recv.at[op, 1 + n],
            device_id=z_id((8, 24)[n]), device_id_type=MESH,
        )

    def farther_copy(buf, op, n):
        block = block_at((24, 8)[n])
        return pltpu.make_async_remote_copy(
            src_ref=buf.at[block, n], dst_ref=buf.at[block, n],
            send_sem=gather_send.at[op, 3 + n], recv_sem=gather_recv.at[op, 3 + n],
            device_id=z_id((8, 24)[n]), device_id_type=MESH,
        )

    def spread_copy(buf, op, k, n):
        block = block_at(SEEDS[k])
        slot = 5 + k * len(SPREAD) + n
        return pltpu.make_async_remote_copy(
            src_ref=buf.at[block], dst_ref=buf.at[block],
            send_sem=gather_send.at[op, slot], recv_sem=gather_recv.at[op, slot],
            device_id=z_id(SPREAD[n]), device_id_type=MESH,
        )

    def spread(buf, op, k):
        for n in range(len(SPREAD)):
            spread_copy(buf, op, k, n).start()

    def gather_opened(buf, op):
        pair_copy(buf, op).wait()
        for n in range(2):
            far_copy(buf, op, n).start()
        spread(buf, op, 0)

    def gather_passed(buf, op):
        for n in range(2):
            far_copy(buf, op, n).wait_recv()
            farther_copy(buf, op, n).start()
        for k in (1, 2):
            spread(buf, op, k)

    def gather_closed(buf, op):
        for n in range(2):
            farther_copy(buf, op, n).wait_recv()
        spread(buf, op, 3)

    def gather_finished(buf, op):
        for k in range(4):
            for n in range(len(SPREAD)):
                spread_copy(buf, op, k, n).wait()
        for n in range(2):
            far_copy(buf, op, n).wait_send()
            farther_copy(buf, op, n).wait_send()

    pair_copy(u_one, 0).start()

    def c_copy(i):
        ty, tq = plane_id(i)
        return pltpu.make_async_remote_copy(
            src_ref=c_ref.at[ty],
            dst_ref=c_all.at[pl.ds(y * 3, 3), pl.ds(pl.multiple_of(q * 16, 16), 16), :],
            send_sem=c_send.at[i], recv_sem=c_recv.at[i],
            device_id=(z * 2 + ty, tq), device_id_type=MESH,
        )

    def s_far(n):
        return pltpu.make_async_remote_copy(
            src_ref=s_ring.at[z], dst_ref=s_ring.at[z],
            send_sem=far_send.at[n], recv_sem=far_recv.at[n],
            device_id=z_id((8, 24)[n]), device_id_type=MESH,
        )

    def s_farther(n):
        half = s_ring.at[block_at((24, 8)[n]), n * 16:n * 16 + 16, :]
        return pltpu.make_async_remote_copy(
            src_ref=half, dst_ref=half,
            send_sem=far_send.at[2 + n], recv_sem=far_recv.at[2 + n],
            device_id=z_id((8, 24)[n]), device_id_type=MESH,
        )

    def hop(k, left, step):
        block = block_at((SEEDS[k] + (step if left else NZ - step)) % NZ)
        slot = k * 7 + (4 if left else 0) + step
        return pltpu.make_async_remote_copy(
            src_ref=s_ring.at[block], dst_ref=s_ring.at[block],
            send_sem=ring_send.at[slot], recv_sem=ring_recv.at[slot],
            device_id=z_id(NZ - 1 if left else 1), device_id_type=MESH,
        )

    def widen(distance):
        block = block_at(distance % NZ)
        rows = s_ring[block].astype(jnp.float32)
        for j in range(4):
            s_wide[j, pl.ds(pl.multiple_of(block * 32, 32), 32), :] = rows[:, j * 128:(j + 1) * 128]

    def hops(k, step):
        return [hop(k, False, step)] + ([hop(k, True, step)] if step < 3 else [])

    def begin(moves):
        for k, step in moves:
            for copy in hops(k, step):
                copy.start()

    def finish(moves):
        for k, step in moves:
            for copy in hops(k, step):
                copy.wait_recv()

    def widen_after(moves):
        for k, step in moves:
            widen(SEEDS[k] - step - 1)
            if step < 3:
                widen(SEEDS[k] + step + 1)

    s_copy.wait()
    for n in range(2):
        s_far(n).start()
    begin([(0, 0)])
    gather_opened(u_one, 0)

    @pl.loop(1, NPLANE)
    def _(i):
        c_copy(i).start()

    widen(0)
    rounds = (
        [(0, 0)],
        [(0, 1)],
        [(0, 2), (1, 0), (2, 0)],
        [(0, 3), (1, 1), (2, 1)],
        [(3, 0), (1, 2), (2, 2)],
        [(3, 1), (1, 3), (2, 3)],
        [(3, 2)],
        [(3, 3)],
    )
    for number, moves in enumerate(rounds):
        if number > 0:
            begin(moves)
            widen_after(rounds[number - 1])
        if number == 2:
            widen(8)
            widen(24)
            gather_passed(u_one, 0)
        if number == 4:
            widen(16)
            gather_closed(u_one, 0)
        finish(moves)
        if number == 1:
            for n in range(2):
                s_far(n).wait_recv()
                s_farther(n).start()
        if number == 3:
            for n in range(2):
                s_farther(n).wait_recv()
    widen_after(rounds[-1])

    @pl.loop(0, 8)
    def _(w):
        for j in range(4):
            s_rows[w, :, j * 128:(j + 1) * 128] = s_wide[j, pl.ds(w, 128, stride=8), :].astype(jnp.bfloat16)

    own_c.wait()

    @pl.loop(1, NPLANE)
    def _(i):
        c_copy(i).wait()

    @pl.loop(0, 6)
    def _(c):
        conduction = c_all[c]
        for w in range(8):
            k_tile[c, :, w * 256:(w + 1) * 256] = lax.dot_general(
                s_rows[w], conduction, (((1,), (1,)), ((), ())), preferred_element_type=jnp.float32
            ).astype(jnp.bfloat16)

    gather_finished(u_one, 0)

    def products(buf, part):
        for block in range(NZ):
            start = (block // 2) * 128 + (block % 2) * 48
            u_wide[start:start + 48, :] = buf[block].astype(jnp.float32).reshape(48, 128)

        for w in range(8):
            u_rows[w * 256:(w + 1) * 256, :] = u_wide[pl.ds(w, 256, stride=8), :].astype(jnp.bfloat16)

        @pl.loop(0, 6)
        def _(c):
            part[c] = jnp.dot(k_tile[c], u_rows[...], preferred_element_type=jnp.float32)

    def sum_copy(part, landing, op, i):
        ty, tq = plane_id(i)
        return pltpu.make_async_remote_copy(
            src_ref=part.at[pl.ds(ty * 3, 3), pl.ds(pl.multiple_of(tq * 8, 8), 8), :],
            dst_ref=landing.at[i],
            send_sem=sum_send.at[op, i], recv_sem=sum_recv.at[op, i],
            device_id=(z * 2 + ty, tq), device_id_type=MESH,
        )

    def reduced(part, landing, op):
        @pl.loop(1, NPLANE)
        def _(i):
            sum_copy(part, landing, op, i).start()

        landing[0] = part[pl.ds(y * 3, 3), pl.ds(pl.multiple_of(q * 8, 8), 8), :]

        @pl.loop(1, NPLANE)
        def _(i):
            sum_copy(part, landing, op, i).wait()

        return jnp.sum(landing[...], axis=0)

    products(u_one, y_part)
    start = u_ref[...].astype(jnp.float32)
    first = ((gaps_ref[...] * start - reduced(y_part, r_one, 0)) / half_width).astype(jnp.bfloat16)
    u_two[z, y] = first
    first_ref[...] = first

    pair_copy(u_two, 1).start()
    gather_opened(u_two, 1)
    gather_passed(u_two, 1)
    gather_closed(u_two, 1)
    gather_finished(u_two, 1)

    products(u_two, y_two)
    second = (gaps_ref[...] * first.astype(jnp.float32) - reduced(y_two, r_two, 1)) / half_width
    filtered_ref[...] = 2.0 * second - start

    for n in range(2):
        s_far(n).wait_send()
        s_farther(n).wait_send()
    for moves in rounds:
        for k, step in moves:
            for copy in hops(k, step):
                copy.wait_send()


def on_device(
    valence_pairs, conduction_pairs, screening, valence_energy, conduction_energy, vectors
):
    gaps = (conduction_energy[:, None] - valence_energy[None, :] - shift_center)[:, :, None]
    gaps = jnp.broadcast_to(gaps, vectors.shape)
    padded = jnp.pad(conduction_pairs, ((0, 0), (0, 4), (0, 0)))
    halves = jnp.transpose(padded.reshape(3, 16, 2, 512), (2, 0, 1, 3))
    in_vmem = pl.BlockSpec(memory_space=pltpu.VMEM)
    bf16, f32 = jnp.bfloat16, jnp.float32
    dma = pltpu.SemaphoreType.DMA
    return pl.pallas_call(
        body,
        out_shape=(
            jax.ShapeDtypeStruct(vectors.shape, bf16),
            jax.ShapeDtypeStruct(vectors.shape, f32),
        ),
        in_specs=[in_vmem, in_vmem, pl.BlockSpec(memory_space=pl.ANY), in_vmem, in_vmem],
        out_specs=(in_vmem, in_vmem),
        scratch_shapes=[
            pltpu.VMEM((1024, 512), bf16),
            pltpu.VMEM((1024, 512), bf16),
            pltpu.VMEM((16, 512), bf16),
            pltpu.VMEM((NZ, 32, 512), bf16),
            pltpu.VMEM((4, 1024, 128), f32),
            pltpu.VMEM((8, 128, 512), bf16),
            pltpu.VMEM((6, 256, 512), bf16),
            pltpu.VMEM((6, 128, 2048), bf16),
            pltpu.VMEM((NZ, 2, 3, 8, 128), bf16),
            pltpu.VMEM((NZ, 2, 3, 8, 128), bf16),
            pltpu.VMEM((2048, 128), f32),
            pltpu.VMEM((2048, 128), bf16),
            pltpu.VMEM((6, 128, 128), f32),
            pltpu.VMEM((6, 128, 128), f32),
            pltpu.VMEM((NPLANE, 3, 8, 128), f32),
            pltpu.VMEM((NPLANE, 3, 8, 128), f32),
            dma((3,)),
            dma((2,)),
            dma((NPLANE,)),
            dma((NPLANE,)),
            dma((4,)),
            dma((4,)),
            dma((28,)),
            dma((28,)),
            dma((2, 33)),
            dma((2, 33)),
            dma((2, NPLANE)),
            dma((2, NPLANE)),
        ],
        compiler_params=pltpu.CompilerParams(collective_id=0, has_side_effects=True),
    )(valence_pairs, halves, screening, gaps, vectors)


def solution(mesh):
    return jax.shard_map(
        on_device,
        mesh=mesh,
        in_specs=(
            P("row", "col", None),
            P("row", "col", None),
            P(),
            P("col"),
            P("row"),
            P("row", "col", None),
        ),
        out_specs=(P("row", "col", None), P("row", "col", None)),
        check_vma=False,
    )
```

```python
import jax
import jax.numpy as jnp
from jax import lax
from jax.experimental import pallas as pl
from jax.experimental.pallas import tpu as pltpu
from jax.sharding import PartitionSpec as P

shift_center = 5.5
half_width = 3.0

NZ = 32
NQ = 16
NPLANE = 32
SEEDS = (0, 24, 8, 16)
SPREAD = (4, 3, 29, 2, 30, 1, 31)
GREETED = (1, 2, 3, 4, 8, 24, 28, 29, 30, 31)
MESH = pl.DeviceIdType.MESH


def body(
    v_ref, c_ref, screening_ref, ve_ref, ce_ref, u_ref,
    first_ref, filtered_ref,
    gaps, c_half, screen_own, screen_other, s_pair, s_ring, s_wide, s_rows, c_all, k_tile,
    u_one, u_two, u_wide, u_rows, y_part, y_two, r_one, r_two,
    local_sem, v_sem, c_send, c_recv, far_send, far_recv, ring_send, ring_recv,
    gather_send, gather_recv, sum_send, sum_recv,
):
    row = lax.axis_index("row")
    q = lax.axis_index("col")
    z = row // 2
    y = row % 2
    me = y * NQ + q

    def plane_id(i):
        p = (me + i) % NPLANE
        return p // NQ, p % NQ

    def z_id(distance):
        return (((z + distance) % NZ) * 2 + y, q)

    def block_at(distance):
        return (z + distance) % NZ

    barrier = pltpu.get_barrier_semaphore()

    for distance in GREETED:
        pl.semaphore_signal(barrier, inc=1, device_id=z_id(distance), device_id_type=MESH)

    @pl.loop(1, NPLANE)
    def _(i):
        ty, tq = plane_id(i)
        pl.semaphore_signal(barrier, inc=1, device_id=(z * 2 + ty, tq), device_id_type=MESH)

    def screen_copy(half, buf, n):
        return pltpu.make_async_copy(
            screening_ref.at[:, pl.ds(pl.multiple_of(half * 512, 512), 512)], buf, local_sem.at[n]
        )

    screen_copy(1 - y, screen_other, 0).start()
    screen_copy(y, screen_own, 1).start()
    c_half[...] = jnp.zeros_like(c_half)
    for half in range(2):
        for c in range(3):
            c_half[half, c, 0:12, :] = c_ref[c, :, half * 512:half * 512 + 512]
    own_c = pltpu.make_async_copy(
        c_half.at[y],
        c_all.at[pl.ds(y * 3, 3), pl.ds(pl.multiple_of(q * 16, 16), 16), :],
        local_sem.at[2],
    )
    own_c.start()
    u_wide[...] = jnp.zeros_like(u_wide)
    state = lax.broadcasted_iota(jnp.int32, (8, 128), 0)
    valence = jnp.zeros((8, 128), jnp.float32)
    for v in range(8):
        valence = jnp.where(state == v, ve_ref[v], valence)
    for c in range(3):
        gaps[c] = ce_ref[c] - valence - shift_center
    u_one[z, y] = u_ref[...]

    raw = v_ref[...].astype(jnp.float32).reshape(16, 1024).astype(jnp.bfloat16)
    own_rows = pl.ds(pl.multiple_of(y * 16, 16), 16)
    screen_copy(1 - y, screen_other, 0).wait()
    s_pair[...] = jnp.dot(raw, screen_other[...], preferred_element_type=jnp.float32).astype(jnp.bfloat16)
    screen_copy(y, screen_own, 1).wait()
    s_ring[z, own_rows, :] = jnp.dot(raw, screen_own[...], preferred_element_type=jnp.float32).astype(
        jnp.bfloat16
    )
    pl.semaphore_wait(barrier, NPLANE - 1 + len(GREETED))

    partner = ((z * 2 + 1 - y), q)
    s_copy = pltpu.make_async_remote_copy(
        src_ref=s_pair, dst_ref=s_ring.at[z, own_rows, :], send_sem=v_sem.at[0], recv_sem=v_sem.at[1],
        device_id=partner, device_id_type=MESH,
    )
    s_copy.start()

    def pair_copy(buf, op):
        return pltpu.make_async_remote_copy(
            src_ref=buf.at[z, y], dst_ref=buf.at[z, y],
            send_sem=gather_send.at[op, 0], recv_sem=gather_recv.at[op, 0],
            device_id=partner, device_id_type=MESH,
        )

    def far_copy(buf, op, n):
        return pltpu.make_async_remote_copy(
            src_ref=buf.at[z], dst_ref=buf.at[z],
            send_sem=gather_send.at[op, 1 + n], recv_sem=gather_recv.at[op, 1 + n],
            device_id=z_id((8, 24)[n]), device_id_type=MESH,
        )

    def farther_copy(buf, op, n):
        block = block_at((24, 8)[n])
        return pltpu.make_async_remote_copy(
            src_ref=buf.at[block, n], dst_ref=buf.at[block, n],
            send_sem=gather_send.at[op, 3 + n], recv_sem=gather_recv.at[op, 3 + n],
            device_id=z_id((8, 24)[n]), device_id_type=MESH,
        )

    def spread_copy(buf, op, k, n):
        block = block_at(SEEDS[k])
        slot = 5 + k * len(SPREAD) + n
        return pltpu.make_async_remote_copy(
            src_ref=buf.at[block], dst_ref=buf.at[block],
            send_sem=gather_send.at[op, slot], recv_sem=gather_recv.at[op, slot],
            device_id=z_id(SPREAD[n]), device_id_type=MESH,
        )

    def spread(buf, op, k):
        for n in range(len(SPREAD)):
            spread_copy(buf, op, k, n).start()

    def gather_opened(buf, op):
        pair_copy(buf, op).wait()
        for n in range(2):
            far_copy(buf, op, n).start()
        spread(buf, op, 0)

    def gather_passed(buf, op):
        for n in range(2):
            far_copy(buf, op, n).wait_recv()
            farther_copy(buf, op, n).start()
        for k in (1, 2):
            spread(buf, op, k)

    def gather_closed(buf, op):
        for n in range(2):
            farther_copy(buf, op, n).wait_recv()
        spread(buf, op, 3)

    def gather_finished(buf, op):
        for k in range(4):
            for n in range(len(SPREAD)):
                spread_copy(buf, op, k, n).wait()
        for n in range(2):
            far_copy(buf, op, n).wait_send()
            farther_copy(buf, op, n).wait_send()

    pair_copy(u_one, 0).start()

    def c_copy(i):
        ty, tq = plane_id(i)
        return pltpu.make_async_remote_copy(
            src_ref=c_half.at[ty],
            dst_ref=c_all.at[pl.ds(y * 3, 3), pl.ds(pl.multiple_of(q * 16, 16), 16), :],
            send_sem=c_send.at[i], recv_sem=c_recv.at[i],
            device_id=(z * 2 + ty, tq), device_id_type=MESH,
        )

    def s_far(n):
        return pltpu.make_async_remote_copy(
            src_ref=s_ring.at[z], dst_ref=s_ring.at[z],
            send_sem=far_send.at[n], recv_sem=far_recv.at[n],
            device_id=z_id((8, 24)[n]), device_id_type=MESH,
        )

    def s_farther(n):
        half = s_ring.at[block_at((24, 8)[n]), n * 16:n * 16 + 16, :]
        return pltpu.make_async_remote_copy(
            src_ref=half, dst_ref=half,
            send_sem=far_send.at[2 + n], recv_sem=far_recv.at[2 + n],
            device_id=z_id((8, 24)[n]), device_id_type=MESH,
        )

    def hop(k, left, step):
        block = block_at((SEEDS[k] + (step if left else NZ - step)) % NZ)
        slot = k * 7 + (4 if left else 0) + step
        return pltpu.make_async_remote_copy(
            src_ref=s_ring.at[block], dst_ref=s_ring.at[block],
            send_sem=ring_send.at[slot], recv_sem=ring_recv.at[slot],
            device_id=z_id(NZ - 1 if left else 1), device_id_type=MESH,
        )

    def widen(distance):
        block = block_at(distance % NZ)
        rows = s_ring[block].astype(jnp.float32)
        for j in range(4):
            s_wide[j, pl.ds(pl.multiple_of(block * 32, 32), 32), :] = rows[:, j * 128:(j + 1) * 128]

    def u_hop(k, left, step):
        block = block_at((SEEDS[k] + (step if left else NZ - step)) % NZ)
        slot = 5 + k * 7 + (4 if left else 0) + step
        return pltpu.make_async_remote_copy(
            src_ref=u_one.at[block], dst_ref=u_one.at[block],
            send_sem=gather_send.at[0, slot], recv_sem=gather_recv.at[0, slot],
            device_id=z_id(NZ - 1 if left else 1), device_id_type=MESH,
        )

    def begin(k, left, step):
        hop(k, left, step).start()
        u_hop(k, left, step).start()

    def pass_on(k, left, step):
        hop(k, left, step).wait_recv()
        u_hop(k, left, step).wait_recv()
        if step < (2 if left else 3):
            begin(k, left, step + 1)

    s_copy.wait()
    pair_copy(u_one, 0).wait()
    for n in range(2):
        s_far(n).start()
        far_copy(u_one, 0, n).start()
    for left in (False, True):
        begin(0, left, 0)

    @pl.loop(1, NPLANE)
    def _(i):
        c_copy(i).start()

    widen(0)
    rounds = (
        [(0, 0)],
        [(0, 1)],
        [(0, 2), (1, 0), (2, 0)],
        [(0, 3), (1, 1), (2, 1)],
        [(1, 2), (2, 2), (3, 0)],
        [(1, 3), (2, 3), (3, 1)],
        [(3, 2)],
        [(3, 3)],
    )
    for number, moves in enumerate(rounds):
        for k, step in moves:
            for left in (False, True)[:2 if step < 3 else 1]:
                pass_on(k, left, step)
        if number == 1:
            for n in range(2):
                s_far(n).wait_recv()
                s_farther(n).start()
                far_copy(u_one, 0, n).wait_recv()
                farther_copy(u_one, 0, n).start()
                for left in (False, True):
                    begin(1 + n, left, 0)
                widen((24, 8)[n])
        if number == 3:
            for n in range(2):
                s_farther(n).wait_recv()
                farther_copy(u_one, 0, n).wait_recv()
            for left in (False, True):
                begin(3, left, 0)
            widen(16)
        for k, step in moves:
            widen(SEEDS[k] - step - 1)
            if step < 3:
                widen(SEEDS[k] + step + 1)

    @pl.loop(0, 8)
    def _(w):
        for j in range(4):
            s_rows[w, :, j * 128:(j + 1) * 128] = s_wide[j, pl.ds(w, 128, stride=8), :].astype(jnp.bfloat16)

    own_c.wait()

    @pl.loop(1, NPLANE)
    def _(i):
        c_copy(i).wait()

    @pl.loop(0, 6)
    def _(c):
        conduction = c_all[c]
        for w in range(8):
            k_tile[c, :, w * 256:(w + 1) * 256] = lax.dot_general(
                s_rows[w], conduction, (((1,), (1,)), ((), ())), preferred_element_type=jnp.float32
            ).astype(jnp.bfloat16)

    def products(buf, part):
        for block in range(NZ):
            start = (block // 2) * 128 + (block % 2) * 48
            u_wide[start:start + 48, :] = buf[block].astype(jnp.float32).reshape(48, 128)

        for w in range(8):
            u_rows[w * 256:(w + 1) * 256, :] = u_wide[pl.ds(w, 256, stride=8), :].astype(jnp.bfloat16)

        @pl.loop(0, 6)
        def _(c):
            part[c] = jnp.dot(k_tile[c], u_rows[...], preferred_element_type=jnp.float32)

    def sum_copy(part, landing, op, i):
        ty, tq = plane_id(i)
        return pltpu.make_async_remote_copy(
            src_ref=part.at[pl.ds(ty * 3, 3), pl.ds(pl.multiple_of(tq * 8, 8), 8), :],
            dst_ref=landing.at[i],
            send_sem=sum_send.at[op, i], recv_sem=sum_recv.at[op, i],
            device_id=(z * 2 + ty, tq), device_id_type=MESH,
        )

    def reduced(part, landing, op):
        @pl.loop(1, NPLANE)
        def _(i):
            sum_copy(part, landing, op, i).start()

        landing[0] = part[pl.ds(y * 3, 3), pl.ds(pl.multiple_of(q * 8, 8), 8), :]

        @pl.loop(1, NPLANE)
        def _(i):
            sum_copy(part, landing, op, i).wait()

        return jnp.sum(landing[...], axis=0)

    products(u_one, y_part)
    start = u_ref[...].astype(jnp.float32)
    first = ((gaps[...] * start - reduced(y_part, r_one, 0)) / half_width).astype(jnp.bfloat16)
    u_two[z, y] = first
    first_ref[...] = first

    pair_copy(u_two, 1).start()
    gather_opened(u_two, 1)
    gather_passed(u_two, 1)
    gather_closed(u_two, 1)
    gather_finished(u_two, 1)

    products(u_two, y_two)
    second = (gaps[...] * first.astype(jnp.float32) - reduced(y_two, r_two, 1)) / half_width
    filtered_ref[...] = 2.0 * second - start

    for n in range(2):
        s_far(n).wait_send()
        s_farther(n).wait_send()
        far_copy(u_one, 0, n).wait_send()
        farther_copy(u_one, 0, n).wait_send()
    for moves in rounds:
        for k, step in moves:
            for left in (False, True)[:2 if step < 3 else 1]:
                hop(k, left, step).wait_send()
                u_hop(k, left, step).wait_send()


def on_device(
    valence_pairs, conduction_pairs, screening, valence_energy, conduction_energy, vectors
):
    in_vmem = pl.BlockSpec(memory_space=pltpu.VMEM)
    in_smem = pl.BlockSpec(memory_space=pltpu.SMEM)
    bf16, f32 = jnp.bfloat16, jnp.float32
    dma = pltpu.SemaphoreType.DMA
    return pl.pallas_call(
        body,
        out_shape=(
            jax.ShapeDtypeStruct(vectors.shape, bf16),
            jax.ShapeDtypeStruct(vectors.shape, f32),
        ),
        in_specs=[in_vmem, in_vmem, pl.BlockSpec(memory_space=pl.ANY), in_smem, in_smem, in_vmem],
        out_specs=(in_vmem, in_vmem),
        scratch_shapes=[
            pltpu.VMEM((3, 8, 128), f32),
            pltpu.VMEM((2, 3, 16, 512), bf16),
            pltpu.VMEM((1024, 512), bf16),
            pltpu.VMEM((1024, 512), bf16),
            pltpu.VMEM((16, 512), bf16),
            pltpu.VMEM((NZ, 32, 512), bf16),
            pltpu.VMEM((4, 1024, 128), f32),
            pltpu.VMEM((8, 128, 512), bf16),
            pltpu.VMEM((6, 256, 512), bf16),
            pltpu.VMEM((6, 128, 2048), bf16),
            pltpu.VMEM((NZ, 2, 3, 8, 128), bf16),
            pltpu.VMEM((NZ, 2, 3, 8, 128), bf16),
            pltpu.VMEM((2048, 128), f32),
            pltpu.VMEM((2048, 128), bf16),
            pltpu.VMEM((6, 128, 128), f32),
            pltpu.VMEM((6, 128, 128), f32),
            pltpu.VMEM((NPLANE, 3, 8, 128), f32),
            pltpu.VMEM((NPLANE, 3, 8, 128), f32),
            dma((3,)),
            dma((2,)),
            dma((NPLANE,)),
            dma((NPLANE,)),
            dma((4,)),
            dma((4,)),
            dma((28,)),
            dma((28,)),
            dma((2, 33)),
            dma((2, 33)),
            dma((2, NPLANE)),
            dma((2, NPLANE)),
        ],
        compiler_params=pltpu.CompilerParams(collective_id=0, has_side_effects=True),
    )(valence_pairs, conduction_pairs, screening, valence_energy, conduction_energy, vectors)


def solution(mesh):
    return jax.shard_map(
        on_device,
        mesh=mesh,
        in_specs=(
            P("row", "col", None),
            P("row", "col", None),
            P(),
            P("col"),
            P("row"),
            P("row", "col", None),
        ),
        out_specs=(P("row", "col", None), P("row", "col", None)),
        check_vma=False,
    )
```

```python
import jax
import jax.numpy as jnp
from jax import lax
from jax.experimental import pallas as pl
from jax.experimental.pallas import tpu as pltpu
from jax.sharding import PartitionSpec as P

shift_center = 5.5
half_width = 3.0

NZ = 32
NQ = 16
NPLANE = 32
SEEDS = (0, 24, 8, 16)
SPREAD = (4, 3, -3, 2, -2, 1, -1)
GREETED = (1, 2, 3, 4, 8, 24, 28, 29, 30, 31)
MESH = pl.DeviceIdType.MESH


def body(
    v_ref, c_ref, screening_ref, ve_ref, ce_ref, u_ref,
    first_ref, filtered_ref,
    gaps, c_half, screen_own, screen_other, s_pair, s_ring, s_wide, s_rows, c_all, k_tile,
    u_one, u_two, u_wide, u_rows, y_part, y_two, r_one, r_two,
    local_sem, v_sem, c_send, c_recv, far_send, far_recv, ring_send, ring_recv,
    gather_send, gather_recv, sum_send, sum_recv,
):
    row = lax.axis_index("row")
    q = lax.axis_index("col")
    z = row // 2
    y = row % 2
    me = y * NQ + q
    side = 1 - 2 * (q % 2)

    def plane_id(i):
        p = (me + i) % NPLANE
        return p // NQ, p % NQ

    def z_id(distance):
        return (((z + distance + NZ) % NZ) * 2 + y, q)

    def block_at(distance):
        return (z + distance + 2 * NZ) % NZ

    barrier = pltpu.get_barrier_semaphore()

    for distance in GREETED:
        pl.semaphore_signal(barrier, inc=1, device_id=z_id(distance), device_id_type=MESH)

    @pl.loop(1, NPLANE)
    def _(i):
        ty, tq = plane_id(i)
        pl.semaphore_signal(barrier, inc=1, device_id=(z * 2 + ty, tq), device_id_type=MESH)

    def screen_copy(half, buf, n):
        return pltpu.make_async_copy(
            screening_ref.at[:, pl.ds(pl.multiple_of(half * 512, 512), 512)], buf, local_sem.at[n]
        )

    screen_copy(1 - y, screen_other, 0).start()
    screen_copy(y, screen_own, 1).start()
    c_half[...] = jnp.zeros_like(c_half)
    for half in range(2):
        for c in range(3):
            c_half[half, c, 0:12, :] = c_ref[c, :, half * 512:half * 512 + 512]
    own_c = pltpu.make_async_copy(
        c_half.at[y],
        c_all.at[pl.ds(y * 3, 3), pl.ds(pl.multiple_of(q * 16, 16), 16), :],
        local_sem.at[2],
    )
    own_c.start()
    u_wide[...] = jnp.zeros_like(u_wide)
    state = lax.broadcasted_iota(jnp.int32, (8, 128), 0)
    valence = jnp.zeros((8, 128), jnp.float32)
    for v in range(8):
        valence = jnp.where(state == v, ve_ref[v], valence)
    for c in range(3):
        gaps[c] = ce_ref[c] - valence - shift_center
    u_one[z, y] = u_ref[...]

    raw = v_ref[...].astype(jnp.float32).reshape(16, 1024).astype(jnp.bfloat16)
    own_rows = pl.ds(pl.multiple_of(y * 16, 16), 16)
    screen_copy(1 - y, screen_other, 0).wait()
    s_pair[...] = jnp.dot(raw, screen_other[...], preferred_element_type=jnp.float32).astype(jnp.bfloat16)
    screen_copy(y, screen_own, 1).wait()
    s_ring[z, own_rows, :] = jnp.dot(raw, screen_own[...], preferred_element_type=jnp.float32).astype(
        jnp.bfloat16
    )
    pl.semaphore_wait(barrier, NPLANE - 1 + len(GREETED))

    partner = ((z * 2 + 1 - y), q)
    s_copy = pltpu.make_async_remote_copy(
        src_ref=s_pair, dst_ref=s_ring.at[z, own_rows, :], send_sem=v_sem.at[0], recv_sem=v_sem.at[1],
        device_id=partner, device_id_type=MESH,
    )
    s_copy.start()

    def pair_copy(buf, op):
        return pltpu.make_async_remote_copy(
            src_ref=buf.at[z, y], dst_ref=buf.at[z, y],
            send_sem=gather_send.at[op, 0], recv_sem=gather_recv.at[op, 0],
            device_id=partner, device_id_type=MESH,
        )

    def far_copy(buf, op, n):
        return pltpu.make_async_remote_copy(
            src_ref=buf.at[z], dst_ref=buf.at[z],
            send_sem=gather_send.at[op, 1 + n], recv_sem=gather_recv.at[op, 1 + n],
            device_id=z_id((8, 24)[n]), device_id_type=MESH,
        )

    def farther_copy(buf, op, n):
        block = block_at((24, 8)[n])
        return pltpu.make_async_remote_copy(
            src_ref=buf.at[block, n], dst_ref=buf.at[block, n],
            send_sem=gather_send.at[op, 3 + n], recv_sem=gather_recv.at[op, 3 + n],
            device_id=z_id((8, 24)[n]), device_id_type=MESH,
        )

    def spread_copy(buf, op, k, n):
        block = block_at(SEEDS[k])
        slot = 5 + k * len(SPREAD) + n
        return pltpu.make_async_remote_copy(
            src_ref=buf.at[block], dst_ref=buf.at[block],
            send_sem=gather_send.at[op, slot], recv_sem=gather_recv.at[op, slot],
            device_id=z_id(side * SPREAD[n]), device_id_type=MESH,
        )

    def spread(buf, op, k):
        for n in range(len(SPREAD)):
            spread_copy(buf, op, k, n).start()

    def gather_opened(buf, op):
        pair_copy(buf, op).wait()
        for n in range(2):
            far_copy(buf, op, n).start()
        spread(buf, op, 0)

    def gather_passed(buf, op):
        for n in range(2):
            far_copy(buf, op, n).wait_recv()
            farther_copy(buf, op, n).start()
        for k in (1, 2):
            spread(buf, op, k)

    def gather_closed(buf, op):
        for n in range(2):
            farther_copy(buf, op, n).wait_recv()
        spread(buf, op, 3)

    def gather_finished(buf, op):
        for k in range(4):
            for n in range(len(SPREAD)):
                spread_copy(buf, op, k, n).wait()
        for n in range(2):
            far_copy(buf, op, n).wait_send()
            farther_copy(buf, op, n).wait_send()

    pair_copy(u_one, 0).start()

    def c_copy(i):
        ty, tq = plane_id(i)
        return pltpu.make_async_remote_copy(
            src_ref=c_half.at[ty],
            dst_ref=c_all.at[pl.ds(y * 3, 3), pl.ds(pl.multiple_of(q * 16, 16), 16), :],
            send_sem=c_send.at[i], recv_sem=c_recv.at[i],
            device_id=(z * 2 + ty, tq), device_id_type=MESH,
        )

    def s_far(n):
        return pltpu.make_async_remote_copy(
            src_ref=s_ring.at[z], dst_ref=s_ring.at[z],
            send_sem=far_send.at[n], recv_sem=far_recv.at[n],
            device_id=z_id((8, 24)[n]), device_id_type=MESH,
        )

    def s_farther(n):
        half = s_ring.at[block_at((24, 8)[n]), n * 16:n * 16 + 16, :]
        return pltpu.make_async_remote_copy(
            src_ref=half, dst_ref=half,
            send_sem=far_send.at[2 + n], recv_sem=far_recv.at[2 + n],
            device_id=z_id((8, 24)[n]), device_id_type=MESH,
        )

    def hop(k, left, step):
        block = block_at(SEEDS[k] + side * (step if left else -step))
        slot = k * 7 + (4 if left else 0) + step
        return pltpu.make_async_remote_copy(
            src_ref=s_ring.at[block], dst_ref=s_ring.at[block],
            send_sem=ring_send.at[slot], recv_sem=ring_recv.at[slot],
            device_id=z_id(side * (-1 if left else 1)), device_id_type=MESH,
        )

    def widen(distance):
        block = block_at(distance)
        rows = s_ring[block].astype(jnp.float32)
        for j in range(4):
            s_wide[j, pl.ds(pl.multiple_of(block * 32, 32), 32), :] = rows[:, j * 128:(j + 1) * 128]

    def u_hop(k, left, step):
        block = block_at(SEEDS[k] + side * (step if left else -step))
        slot = 5 + k * 7 + (4 if left else 0) + step
        return pltpu.make_async_remote_copy(
            src_ref=u_one.at[block], dst_ref=u_one.at[block],
            send_sem=gather_send.at[0, slot], recv_sem=gather_recv.at[0, slot],
            device_id=z_id(side * (-1 if left else 1)), device_id_type=MESH,
        )

    def begin(k, left, step):
        hop(k, left, step).start()
        u_hop(k, left, step).start()

    def pass_on(k, left, step):
        hop(k, left, step).wait_recv()
        u_hop(k, left, step).wait_recv()
        if step < (2 if left else 3):
            begin(k, left, step + 1)

    s_copy.wait()
    pair_copy(u_one, 0).wait()
    for n in range(2):
        s_far(n).start()
        far_copy(u_one, 0, n).start()
    for left in (False, True):
        begin(0, left, 0)

    @pl.loop(1, NPLANE)
    def _(i):
        c_copy(i).start()

    widen(0)
    rounds = (
        [(0, 0)],
        [(0, 1)],
        [(0, 2), (1, 0), (2, 0)],
        [(0, 3), (1, 1), (2, 1)],
        [(1, 2), (2, 2), (3, 0)],
        [(1, 3), (2, 3), (3, 1)],
        [(3, 2)],
        [(3, 3)],
    )
    for number, moves in enumerate(rounds):
        for k, step in moves:
            for left in (False, True)[:2 if step < 3 else 1]:
                pass_on(k, left, step)
        if number == 1:
            for n in range(2):
                s_far(n).wait_recv()
                s_farther(n).start()
                far_copy(u_one, 0, n).wait_recv()
                farther_copy(u_one, 0, n).start()
                for left in (False, True):
                    begin(1 + n, left, 0)
                widen((24, 8)[n])
        if number == 3:
            for n in range(2):
                s_farther(n).wait_recv()
                farther_copy(u_one, 0, n).wait_recv()
            for left in (False, True):
                begin(3, left, 0)
            widen(16)
        for k, step in moves:
            widen(SEEDS[k] - side * (step + 1))
            if step < 3:
                widen(SEEDS[k] + side * (step + 1))

    @pl.loop(0, 8)
    def _(w):
        for j in range(4):
            s_rows[w, :, j * 128:(j + 1) * 128] = s_wide[j, pl.ds(w, 128, stride=8), :].astype(jnp.bfloat16)

    own_c.wait()

    @pl.loop(1, NPLANE)
    def _(i):
        c_copy(i).wait()

    @pl.loop(0, 6)
    def _(c):
        conduction = c_all[c]
        for w in range(8):
            k_tile[c, :, w * 256:(w + 1) * 256] = lax.dot_general(
                s_rows[w], conduction, (((1,), (1,)), ((), ())), preferred_element_type=jnp.float32
            ).astype(jnp.bfloat16)

    def products(buf, part):
        for block in range(NZ):
            start = (block // 2) * 128 + (block % 2) * 48
            u_wide[start:start + 48, :] = buf[block].astype(jnp.float32).reshape(48, 128)

        for w in range(8):
            u_rows[w * 256:(w + 1) * 256, :] = u_wide[pl.ds(w, 256, stride=8), :].astype(jnp.bfloat16)

        @pl.loop(0, 6)
        def _(c):
            part[c] = jnp.dot(k_tile[c], u_rows[...], preferred_element_type=jnp.float32)

    def sum_copy(part, landing, op, i):
        ty, tq = plane_id(i)
        return pltpu.make_async_remote_copy(
            src_ref=part.at[pl.ds(ty * 3, 3), pl.ds(pl.multiple_of(tq * 8, 8), 8), :],
            dst_ref=landing.at[i],
            send_sem=sum_send.at[op, i], recv_sem=sum_recv.at[op, i],
            device_id=(z * 2 + ty, tq), device_id_type=MESH,
        )

    def reduced(part, landing, op):
        @pl.loop(1, NPLANE)
        def _(i):
            sum_copy(part, landing, op, i).start()

        landing[0] = part[pl.ds(y * 3, 3), pl.ds(pl.multiple_of(q * 8, 8), 8), :]

        @pl.loop(1, NPLANE)
        def _(i):
            sum_copy(part, landing, op, i).wait()

        return jnp.sum(landing[...], axis=0)

    products(u_one, y_part)
    start = u_ref[...].astype(jnp.float32)
    first = ((gaps[...] * start - reduced(y_part, r_one, 0)) / half_width).astype(jnp.bfloat16)
    u_two[z, y] = first
    first_ref[...] = first

    pair_copy(u_two, 1).start()
    gather_opened(u_two, 1)
    gather_passed(u_two, 1)
    gather_closed(u_two, 1)
    gather_finished(u_two, 1)

    products(u_two, y_two)
    second = (gaps[...] * first.astype(jnp.float32) - reduced(y_two, r_two, 1)) / half_width
    filtered_ref[...] = 2.0 * second - start

    for n in range(2):
        s_far(n).wait_send()
        s_farther(n).wait_send()
        far_copy(u_one, 0, n).wait_send()
        farther_copy(u_one, 0, n).wait_send()
    for moves in rounds:
        for k, step in moves:
            for left in (False, True)[:2 if step < 3 else 1]:
                hop(k, left, step).wait_send()
                u_hop(k, left, step).wait_send()


def on_device(
    valence_pairs, conduction_pairs, screening, valence_energy, conduction_energy, vectors
):
    in_vmem = pl.BlockSpec(memory_space=pltpu.VMEM)
    in_smem = pl.BlockSpec(memory_space=pltpu.SMEM)
    bf16, f32 = jnp.bfloat16, jnp.float32
    dma = pltpu.SemaphoreType.DMA
    return pl.pallas_call(
        body,
        out_shape=(
            jax.ShapeDtypeStruct(vectors.shape, bf16),
            jax.ShapeDtypeStruct(vectors.shape, f32),
        ),
        in_specs=[in_vmem, in_vmem, pl.BlockSpec(memory_space=pl.ANY), in_smem, in_smem, in_vmem],
        out_specs=(in_vmem, in_vmem),
        scratch_shapes=[
            pltpu.VMEM((3, 8, 128), f32),
            pltpu.VMEM((2, 3, 16, 512), bf16),
            pltpu.VMEM((1024, 512), bf16),
            pltpu.VMEM((1024, 512), bf16),
            pltpu.VMEM((16, 512), bf16),
            pltpu.VMEM((NZ, 32, 512), bf16),
            pltpu.VMEM((4, 1024, 128), f32),
            pltpu.VMEM((8, 128, 512), bf16),
            pltpu.VMEM((6, 256, 512), bf16),
            pltpu.VMEM((6, 128, 2048), bf16),
            pltpu.VMEM((NZ, 2, 3, 8, 128), bf16),
            pltpu.VMEM((NZ, 2, 3, 8, 128), bf16),
            pltpu.VMEM((2048, 128), f32),
            pltpu.VMEM((2048, 128), bf16),
            pltpu.VMEM((6, 128, 128), f32),
            pltpu.VMEM((6, 128, 128), f32),
            pltpu.VMEM((NPLANE, 3, 8, 128), f32),
            pltpu.VMEM((NPLANE, 3, 8, 128), f32),
            dma((3,)),
            dma((2,)),
            dma((NPLANE,)),
            dma((NPLANE,)),
            dma((4,)),
            dma((4,)),
            dma((28,)),
            dma((28,)),
            dma((2, 33)),
            dma((2, 33)),
            dma((2, NPLANE)),
            dma((2, NPLANE)),
        ],
        compiler_params=pltpu.CompilerParams(collective_id=0, has_side_effects=True),
    )(valence_pairs, conduction_pairs, screening, valence_energy, conduction_energy, vectors)


def solution(mesh):
    return jax.shard_map(
        on_device,
        mesh=mesh,
        in_specs=(
            P("row", "col", None),
            P("row", "col", None),
            P(),
            P("col"),
            P("row"),
            P("row", "col", None),
        ),
        out_specs=(P("row", "col", None), P("row", "col", None)),
        check_vma=False,
    )
```
